32 devices in a mesh: dom: 32 (over z, y, x, core).
Axes of the slice: x: 2, y: 2, z: 4, core: 2. Of those that a mesh axis runs over, the one named last changes fastest.
Arguments:
- vectors: bfloat16 [64, 131072], P(None, 'dom')
- diag_tiles: bfloat16 [1024, 128, 128], P('dom'), as said below
- pair_tiles: bfloat16 [3072, 2, 128, 128], P('dom'), as said below
- halo_tiles: bfloat16 [1024, 128, 128], P('dom'), as said below
- halo_rows: int32 [32, 32], P('dom'), may hold values from 1 to 31, as said below
- pair_index: int32 [32, 96, 2], P('dom'), may hold values from 0 to 31, as said below
- pair_count: int32 [32], P('dom'), may hold values from 24 to 96, as said below
Outputs:
- basis: bfloat16 [64, 131072], P(None, 'dom')
- ritz: float32 [64, 64], replicated
The draws below stay inside these ranges and needn't reach their ends.
Inputs may be any that keep to these rules, and one draw needn't show every extreme that they name: `diag_tiles`: each tile is symmetric. `pair_tiles`: entry [j, 1] is the transpose of entry [j, 0]. `halo_tiles`: entry d * 32 + p is the transpose of entry p * 32 + d. `halo_rows`: no entry is a multiple of 4. `pair_index`: the 96 entries of a partition are distinct pairs (r, c) with r < c. The first pair_count[d] entries of pair_index[d] are live; some partition has 96.
All inputs are finite; a program needn't handle non-finite values.
Results may differ from the reference program's by a relative error of at most 0.023.
Values may be sent and summed in bfloat16 or wider, within the bound.
A program may use at most 128 MiB of HBM per device.

```python
import math
import jax
import jax.numpy as jnp
import numpy as np
from jax import lax

K = 64
B = 128
BD = 32
DEGREE = 4
EMAX = 96
PEERS = 32
ROWS = 131072


def tile_scale():
    return 0.5 / math.sqrt(B * (1.0 + 1.2 * EMAX / BD + PEERS / BD))


def tile_noise(key, shape):
    return jax.random.normal(key, shape, jnp.float32)


def draw_vectors(key, part):
    key_base = jax.random.fold_in(jax.random.fold_in(key, 11), 0)
    key_mix = jax.random.fold_in(jax.random.fold_in(key, 11), 1)
    key_common = jax.random.fold_in(jax.random.fold_in(key, 11), 3)
    normal_draw = jax.random.normal(key_base, (K, ROWS), jnp.float32)
    common_row = jax.random.normal(key_common, (1, ROWS), jnp.float32)
    normal_draw = normal_draw + 2.5 * common_row
    mixing = jnp.eye(K, dtype=jnp.float32) + 0.3 * jax.random.normal(key_mix, (K, K), jnp.float32) / math.sqrt(K)
    return jnp.dot(mixing, normal_draw).astype(jnp.bfloat16)


def draw_diag_tiles(key, part):
    normal_draw = tile_noise(jax.random.fold_in(key, 21), (PEERS * BD, B, B))
    symmetric = (normal_draw + jnp.swapaxes(normal_draw, 1, 2)) * (tile_scale() / math.sqrt(2.0))
    position = (jnp.arange(PEERS * BD) // BD).astype(jnp.float32) / max(PEERS - 1, 1)
    block_place = jnp.arange(PEERS * BD) % BD
    rough = jax.random.uniform(jax.random.fold_in(key, 22), (PEERS * BD,), jnp.float32, 0.0, 1.0)
    upper_shift = 0.3 + 0.3 * rough + 0.2 * position
    shift = jnp.where(block_place % 4 == 0, 0.05, upper_shift)
    symmetric = symmetric + shift[:, None, None] * jnp.eye(B, dtype=jnp.float32)[None, :, :]
    return symmetric.astype(jnp.bfloat16)


def draw_pair_tiles(key, part):
    normal_draw = tile_noise(jax.random.fold_in(key, 31), (PEERS * EMAX, B, B)) * tile_scale()
    return jnp.stack([normal_draw, jnp.swapaxes(normal_draw, 1, 2)], axis=1).astype(jnp.bfloat16)


def draw_halo_tiles(key, part):
    normal_draw = tile_noise(jax.random.fold_in(key, 41), (PEERS, PEERS, B, B)) * tile_scale()
    mirrored = jnp.swapaxes(jnp.swapaxes(normal_draw, 0, 1), 2, 3)
    own_ids = jnp.arange(PEERS)[:, None, None, None]
    peer_ids = jnp.arange(PEERS)[None, :, None, None]
    symmetric = jnp.where(own_ids < peer_ids, normal_draw, jnp.where(own_ids > peer_ids, mirrored, (normal_draw + mirrored) / math.sqrt(2.0)))
    return symmetric.reshape(PEERS * PEERS, B, B).astype(jnp.bfloat16)


def draw_halo_rows(key, part):
    key_group, key_offset, key_spot = jax.random.split(jax.random.fold_in(key, 71), 3)
    groups = jax.random.randint(key_group, (PEERS * PEERS,), 0, BD // 4)
    offsets = jax.random.randint(key_offset, (PEERS * PEERS,), 1, 4)
    values = 4 * groups + offsets
    spot = jax.random.randint(key_spot, (), 0, PEERS * PEERS)
    flat_iota = jnp.arange(PEERS * PEERS)
    values = jnp.where(flat_iota == spot, 1, values)
    values = jnp.where(flat_iota == (spot + 1) % (PEERS * PEERS), BD - 1, values)
    return values.reshape(PEERS, PEERS).astype(jnp.int32)


def draw_pair_index(key, part):
    first_rows, second_cols = np.triu_indices(BD, 1)
    pair_total = BD * (BD - 1) // 2
    scores = jax.random.randint(jax.random.fold_in(key, 51), (PEERS, pair_total), 0, 1 << 16) * pair_total + jnp.arange(pair_total)[None, :]
    chosen = jnp.argsort(scores, axis=1)[:, :EMAX]
    row_ids = jnp.asarray(first_rows, jnp.int32)[chosen]
    col_ids = jnp.asarray(second_cols, jnp.int32)[chosen]
    return jnp.stack([row_ids, col_ids], axis=-1).astype(jnp.int32)


def draw_pair_count(key, part):
    key_level, key_busy = jax.random.split(jax.random.fold_in(key, 61))
    levels = jax.random.randint(key_level, (PEERS,), 0, 3)
    counts = EMAX // jnp.left_shift(jnp.ones((PEERS,), jnp.int32), levels)
    busiest = jax.random.randint(key_busy, (), 0, PEERS)
    return jnp.where(jnp.arange(PEERS) == busiest, EMAX, counts).astype(jnp.int32)


def setup_inputs(seed: int = 0) -> dict:
    seeds = jax.random.split(jax.random.key(seed), 8)
    return {
        "vectors": draw_vectors(jax.random.fold_in(seeds[7], 71), 0),
        "diag_tiles": draw_diag_tiles(jax.random.fold_in(seeds[7], 71), 0),
        "pair_tiles": draw_pair_tiles(jax.random.fold_in(seeds[7], 71), 0),
        "halo_tiles": draw_halo_tiles(jax.random.fold_in(seeds[7], 71), 0),
        "halo_rows": draw_halo_rows(jax.random.fold_in(seeds[7], 71), 0),
        "pair_index": draw_pair_index(jax.random.fold_in(seeds[7], 71), 0),
        "pair_count": draw_pair_count(jax.random.fold_in(seeds[7], 71), 0),
    }


first_centre = -0.5

def apply_matrix(current, diag_tiles, pair_tiles, halo_tiles, halo_rows, pair_index, pair_count):
    blocked = current.astype(jnp.float32).reshape(K, PEERS, BD, B)
    diag_all = diag_tiles.reshape(PEERS, BD, B, B)
    pair_all = pair_tiles.reshape(PEERS, EMAX, 2, B, B)
    halo_all = halo_tiles.reshape(PEERS, PEERS, B, B)
    block_iota = jnp.arange(BD)

    def device_terms(device):
        own = blocked[:, device]
        result = jnp.einsum('krj,rij->kri', own, diag_all[device].astype(jnp.float32))
        row_ids = pair_index[device, :, 0]
        col_ids = pair_index[device, :, 1]
        live_mask = (jnp.arange(EMAX) < pair_count[device]).astype(jnp.float32)
        tiles_here = pair_all[device].astype(jnp.float32)
        upper_terms = jnp.einsum('kej,eij->kei', own[:, col_ids], tiles_here[:, 0])
        lower_terms = jnp.einsum('kej,eij->kei', own[:, row_ids], tiles_here[:, 1])
        onehot_first = (row_ids[:, None] == block_iota[None, :]).astype(jnp.float32) * live_mask[:, None]
        onehot_second = (col_ids[:, None] == block_iota[None, :]).astype(jnp.float32) * live_mask[:, None]
        result = result + jnp.einsum('kei,er->kri', upper_terms, onehot_first)
        result = result + jnp.einsum('kei,er->kri', lower_terms, onehot_second)
        sources = blocked[:, jnp.arange(PEERS), halo_rows[:, device]]
        products = jnp.einsum('kpj,pij->kpi', sources, halo_all[device].astype(jnp.float32))
        onehot_halo = (halo_rows[device][:, None] == block_iota[None, :]).astype(jnp.float32)
        return result + jnp.einsum('kpi,pr->kri', products, onehot_halo)
    stacked = lax.map(device_terms, jnp.arange(PEERS))
    return jnp.transpose(stacked, (1, 0, 2, 3)).reshape(K, ROWS)

def subspace_step(start, first, centre, operator):
    previous = start
    current = (first - centre * start.astype(jnp.float32)).astype(jnp.bfloat16)
    for degree in range(DEGREE - 1):
        applied = operator(current)
        following = (2.0 * (applied - centre * current.astype(jnp.float32)) - previous.astype(jnp.float32)).astype(jnp.bfloat16)
        previous, current = (current, following)
    gram_matrix = jnp.dot(current.astype(jnp.float32), current.T.astype(jnp.float32), preferred_element_type=jnp.float32) / ROWS
    chol_lower = jnp.linalg.cholesky(gram_matrix)
    inverse = jax.scipy.linalg.solve_triangular(chol_lower, jnp.eye(K, dtype=jnp.float32), lower=True)
    following = jnp.dot(inverse, current.astype(jnp.float32), precision=lax.Precision.HIGHEST).astype(jnp.bfloat16)
    applied = operator(following)
    projected = jnp.dot(following.astype(jnp.float32), applied.T, precision=lax.Precision.HIGHEST) / ROWS
    return (following, applied, projected)

def reference(vectors, diag_tiles, pair_tiles, halo_tiles, halo_rows, pair_index, pair_count):

    def operator(current):
        return apply_matrix(current, diag_tiles, pair_tiles, halo_tiles, halo_rows, pair_index, pair_count)
    first = operator(vectors)
    basis_one, image_one, projected_one = subspace_step(vectors, first, first_centre, operator)
    centre_two = jnp.trace(projected_one) / K - 1.0
    basis, image_two, ritz = subspace_step(basis_one, image_one, centre_two, operator)
    return (basis, ritz)
```

```python
import functools

import jax
import jax.numpy as jnp
from jax import lax
from jax.experimental import pallas as pl
from jax.experimental.pallas import tpu as pltpu
from jax.sharding import PartitionSpec as P

DEGREE = 4
FIRST_CENTRE = -0.5
MESH = pl.DeviceIdType.MESH
f32 = jnp.float32
bf16 = jnp.bfloat16


def nt_dot(a, b):
    return lax.dot_general(a, b, (((1,), (1,)), ((), ())), preferred_element_type=f32)


def kernel(
    n,
    total_rows,
    tile_id,
    source_id,
    keep,
    end_of,
    send_rows,
    halo_order,
    halo_keep,
    halo_end,
    halo_any,
    vec_ref,
    diag_hbm,
    pair_hbm,
    halo_hbm,
    basis_ref,
    ritz_ref,
    tiles,
    halo_tiles,
    y_buf,
    image,
    partial,
    halo_part,
    stage,
    arrived_even,
    arrived_odd,
    red_out,
    red_in,
    load_sem,
    send_sem,
    recv_sem,
    red_send,
    red_recv,
):
    me = lax.axis_index("dom")
    k, width = vec_ref.shape
    blocks = y_buf.shape[1]
    b = width // blocks
    entries = tiles.shape[0]
    pairs2 = entries - blocks

    loads = [
        pltpu.make_async_copy(diag_hbm, tiles.at[pl.ds(0, blocks)], load_sem.at[0]),
        pltpu.make_async_copy(pair_hbm, tiles.at[pl.ds(blocks, pairs2)], load_sem.at[1]),
        pltpu.make_async_copy(halo_hbm, halo_tiles, load_sem.at[2]),
    ]
    for load in loads:
        load.start()

    barrier = pltpu.get_barrier_semaphore()

    def greet(s, _):
        pl.semaphore_signal(
            barrier, inc=1, device_id=(lax.rem(me + s, n),), device_id_type=MESH
        )
        return 0

    lax.fori_loop(1, n, greet, 0)
    for j in range(blocks):
        y_buf[0, j] = vec_ref[:, j * b : (j + 1) * b]
    pl.semaphore_wait(barrier, n - 1)

    slots = (arrived_even, arrived_odd)

    def halo_copy(slot, peer_from, peer_to):
        return pltpu.make_async_remote_copy(
            src_ref=stage.at[peer_to],
            dst_ref=slots[slot].at[peer_from],
            send_sem=send_sem.at[peer_to],
            recv_sem=recv_sem.at[slot, peer_from],
            device_id=(peer_to,),
            device_id_type=MESH,
        )

    entry_unroll = next(u for u in (8, 4, 2, 1) if entries % u == 0)
    halo_unroll = next(u for u in (8, 4, 2, 1) if n % u == 0)

    def operator(count, cur):
        slot = count % 2
        arrived = slots[slot]

        def send(s, _):
            peer = lax.rem(me + s, n)
            stage[peer] = y_buf[cur, send_rows[peer]]
            halo_copy(slot, me, peer).start()
            return 0

        lax.fori_loop(1, n, send, 0)
        arrived[me] = y_buf[cur, send_rows[me]]
        if count == 0:
            for load in loads:
                load.wait()

        def local(i, carry):
            for u in range(entry_unroll):
                e = i * entry_unroll + u
                product = jnp.dot(
                    y_buf[cur, source_id[e]], tiles[tile_id[e]], preferred_element_type=f32
                )
                carry = carry * keep[e] + product
                partial[e] = carry
            return carry

        lax.fori_loop(0, entries // entry_unroll, local, jnp.zeros((k, b), f32))

        def receive(s, _):
            peer = lax.rem(me + n - s, n)
            halo_copy(slot, peer, peer).wait_recv()
            return 0

        lax.fori_loop(1, n, receive, 0)

        def halo(i, carry):
            for u in range(halo_unroll):
                e = i * halo_unroll + u
                p = halo_order[e]
                carry = carry * halo_keep[e] + nt_dot(arrived[p], halo_tiles[p])
                halo_part[e] = carry
            return carry

        lax.fori_loop(0, n // halo_unroll, halo, jnp.zeros((k, b), f32))

        def sent(s, _):
            halo_copy(slot, me, lax.rem(me + s, n)).wait_send()
            return 0

        lax.fori_loop(1, n, sent, 0)

    def applied(r):
        return partial[end_of[r]] + halo_part[halo_end[r]] * halo_any[r]

    def over_blocks(body, init, unroll=4):
        def step(i, carry):
            for u in range(unroll):
                carry = body(i * unroll + u, carry)
            return carry

        if blocks % unroll:
            return lax.fori_loop(0, blocks, body, init)
        return lax.fori_loop(0, blocks // unroll, step, init)

    def reduce_sum(value):
        rows = value.shape[0]
        red_out[0:rows] = value
        red_in[me, 0:rows] = value

        def copy(peer_from, peer_to):
            return pltpu.make_async_remote_copy(
                src_ref=red_out.at[pl.ds(0, rows)],
                dst_ref=red_in.at[peer_from, pl.ds(0, rows)],
                send_sem=red_send.at[peer_to],
                recv_sem=red_recv.at[peer_from],
                device_id=(peer_to,),
                device_id_type=MESH,
            )

        def send(s, _):
            copy(me, lax.rem(me + s, n)).start()
            return 0

        def receive(s, _):
            peer = lax.rem(me + n - s, n)
            copy(peer, peer).wait_recv()
            return 0

        def sent(s, _):
            copy(me, lax.rem(me + s, n)).wait_send()
            return 0

        lax.fori_loop(1, n, send, 0)
        lax.fori_loop(1, n, receive, 0)
        total = lax.fori_loop(
            0, n, lambda p, acc: acc + red_in[p, 0:rows], jnp.zeros_like(value)
        )
        lax.fori_loop(1, n, sent, 0)
        return total

    half = k // 2
    lane = lax.broadcasted_iota(jnp.int32, (half, 2 * k), 1)

    def pack(doubled):
        return jnp.where(lane < k, doubled[:half], doubled[half:])

    def unpack(packed):
        return jnp.concatenate([packed, pltpu.roll(packed, k, 1)], axis=0)

    def inverse_factor(gram):
        sub = 8
        lanes = lax.broadcasted_iota(jnp.int32, (sub, 2 * k), 1)
        rows = lax.broadcasted_iota(jnp.int32, (sub, 2 * k), 0)
        sub_row = lax.broadcasted_iota(jnp.int32, (sub, 1), 0)
        parts = []
        for t in range(k // sub):
            unit = (lanes == rows + (t * sub + k)).astype(f32)
            parts.append(jnp.where(lanes < k, gram[t * sub : (t + 1) * sub], unit))
        for j in range(k):
            t0, r0 = divmod(j, sub)
            row = parts[t0][r0 : r0 + 1, :]
            scaled = row / row[:, j : j + 1]
            for t in range(t0, k // sub):
                column = parts[t][:, j : j + 1]
                if t == t0:
                    column = jnp.where(sub_row > r0, column, 0.0)
                parts[t] = parts[t] - column * scaled
        for t in range(k // sub):
            pivot = jnp.sum(
                jnp.where(lanes == rows + t * sub, parts[t], 0.0), axis=1, keepdims=True
            )
            parts[t] = parts[t] * lax.rsqrt(pivot)
        return pltpu.roll(jnp.concatenate(parts, axis=0), k, 1)[:, :k]

    def subspace_step(count, start, centre, last):
        def first_update(r, _):
            value = image[r] - centre * y_buf[start, r].astype(f32)
            y_buf[(start + 1) % 3, r] = value.astype(bf16)
            return 0

        over_blocks(first_update, 0)
        previous, current = start, (start + 1) % 3
        for _ in range(DEGREE - 1):
            operator(count, current)
            count += 1
            following = (current + 1) % 3

            def update(r, _, previous=previous, current=current, following=following):
                value = 2.0 * (applied(r) - centre * y_buf[current, r].astype(f32))
                value = value - y_buf[previous, r].astype(f32)
                y_buf[following, r] = value.astype(bf16)
                return 0

            over_blocks(update, 0)
            previous, current = current, following

        def gram_term(r, acc):
            block = y_buf[current, r]
            return acc + nt_dot(block, jnp.concatenate([block, block], axis=0))

        doubled = over_blocks(gram_term, jnp.zeros((k, 2 * k), f32))
        gram = unpack(reduce_sum(pack(doubled))) / total_rows
        inverse = inverse_factor(gram)
        high = inverse.astype(bf16)
        rest = inverse - high.astype(f32)
        middle = rest.astype(bf16)
        low = (rest - middle.astype(f32)).astype(bf16)
        left = jnp.concatenate([high, middle, low], axis=1)
        result = (current + 1) % 3

        def orthonormal(r, _):
            block = y_buf[current, r]
            stacked = jnp.concatenate([block, block, block], axis=0)
            y_buf[result, r] = jnp.dot(left, stacked, preferred_element_type=f32).astype(bf16)
            return 0

        over_blocks(orthonormal, 0)
        operator(count, result)
        count += 1
        if not last:

            def keep_image(r, acc):
                value = applied(r)
                image[r] = value
                return acc + value * y_buf[result, r].astype(f32)

            traced = over_blocks(keep_image, jnp.zeros((k, b), f32))
            traced = sum(traced[t * 8 : (t + 1) * 8] for t in range(k // 8))
            traced = reduce_sum(traced)
            traced = jnp.sum(jnp.sum(traced, axis=1, keepdims=True), axis=0, keepdims=True)
            return count, result, traced / total_rows

        def ritz_term(r, acc):
            value = applied(r)
            top = value.astype(bf16)
            bottom = (value - top.astype(f32)).astype(bf16)
            return acc + nt_dot(y_buf[result, r], jnp.concatenate([top, bottom], axis=0))

        doubled = over_blocks(ritz_term, jnp.zeros((k, 2 * k), f32))
        doubled = doubled + pltpu.roll(doubled, k, 1)
        ritz_ref[...] = unpack(reduce_sum(pack(doubled)))[:, :k] / total_rows
        for j in range(blocks):
            basis_ref[:, j * b : (j + 1) * b] = y_buf[result, j]
        return count, result, None

    operator(0, 0)

    def keep_first(r, _):
        image[r] = applied(r)
        return 0

    over_blocks(keep_first, 0)
    count, result, trace = subspace_step(1, 0, FIRST_CENTRE, False)
    subspace_step(count, result, trace / k - 1.0, True)


def sorted_order(keys):
    count = keys.shape[0]
    ids = jnp.arange(count)
    before = (keys[None, :] < keys[:, None]) | (
        (keys[None, :] == keys[:, None]) & (ids[None, :] < ids[:, None])
    )
    rank = jnp.sum(before.astype(jnp.int32), axis=1)
    return (rank[:, None] == ids[None, :]).astype(jnp.int32)


def place(onehot, values):
    return jnp.sum(onehot * values[:, None], axis=0).astype(jnp.int32)


def local(vectors, diag_tiles, pair_tiles, halo_tiles, halo_rows, pair_index, pair_count):
    n = lax.axis_size("dom")
    k, width = vectors.shape
    blocks, b = diag_tiles.shape[0], diag_tiles.shape[1]
    pairs = pair_tiles.shape[0]
    entries = blocks + 2 * pairs
    row_ids, col_ids = pair_index[0, :, 0], pair_index[0, :, 1]
    live = jnp.arange(pairs) < pair_count[0]
    block_ids = jnp.arange(blocks)
    pair_ids = jnp.arange(pairs)
    target = jnp.concatenate(
        [block_ids, jnp.where(live, row_ids, blocks), jnp.where(live, col_ids, blocks)]
    )
    source = jnp.concatenate([block_ids, col_ids, row_ids])
    tile = jnp.concatenate([block_ids, blocks + 2 * pair_ids + 1, blocks + 2 * pair_ids])
    onehot = sorted_order(target)
    tile_id, source_id = place(onehot, tile), place(onehot, source)
    keep = (tile_id >= blocks).astype(f32)
    end_of = jnp.sum((target[None, :] <= block_ids[:, None]).astype(jnp.int32), axis=1) - 1
    rows = halo_rows[0]
    halo_onehot = sorted_order(rows)
    halo_order = place(halo_onehot, jnp.arange(n))
    halo_sorted = place(halo_onehot, rows)
    halo_keep = jnp.concatenate(
        [jnp.zeros((1,), f32), (halo_sorted[1:] == halo_sorted[:-1]).astype(f32)]
    )
    upto = jnp.sum((rows[None, :] <= block_ids[:, None]).astype(jnp.int32), axis=1)
    halo_any = jnp.any(rows[None, :] == block_ids[:, None], axis=1).astype(f32)
    halo_end = jnp.maximum(upto - 1, 0)

    smem = pl.BlockSpec(memory_space=pltpu.SMEM)
    vmem = pl.BlockSpec(memory_space=pltpu.VMEM)
    hbm = pl.BlockSpec(memory_space=pl.ANY)
    return pl.pallas_call(
        functools.partial(kernel, n, float(width * n)),
        out_shape=(
            jax.ShapeDtypeStruct((k, width), bf16),
            jax.ShapeDtypeStruct((k, k), f32),
        ),
        in_specs=[smem] * 9 + [vmem, hbm, hbm, hbm],
        out_specs=(vmem, vmem),
        scratch_shapes=[
            pltpu.VMEM((entries, b, b), bf16),
            pltpu.VMEM((n, b, b), bf16),
            pltpu.VMEM((3, blocks, k, b), bf16),
            pltpu.VMEM((blocks, k, b), f32),
            pltpu.VMEM((entries, k, b), f32),
            pltpu.VMEM((n, k, b), f32),
            pltpu.VMEM((n, k, b), bf16),
            pltpu.VMEM((n, k, b), bf16),
            pltpu.VMEM((n, k, b), bf16),
            pltpu.VMEM((k // 2, 2 * k), f32),
            pltpu.VMEM((n, k // 2, 2 * k), f32),
            pltpu.SemaphoreType.DMA((3,)),
            pltpu.SemaphoreType.DMA((n,)),
            pltpu.SemaphoreType.DMA((2, n)),
            pltpu.SemaphoreType.DMA((n,)),
            pltpu.SemaphoreType.DMA((n,)),
        ],
        compiler_params=pltpu.CompilerParams(
            collective_id=0, has_side_effects=True, vmem_limit_bytes=48 * 1024 * 1024
        ),
    )(
        tile_id,
        source_id,
        keep,
        end_of,
        rows,
        halo_order,
        halo_keep,
        halo_end,
        halo_any,
        vectors,
        diag_tiles,
        pair_tiles.reshape(2 * pairs, b, b),
        halo_tiles,
    )


def solution(mesh):
    return jax.shard_map(
        local,
        mesh=mesh,
        in_specs=(
            P(None, "dom"),
            P("dom", None, None),
            P("dom", None, None, None),
            P("dom", None, None),
            P("dom", None),
            P("dom", None, None),
            P("dom"),
        ),
        out_specs=(P(None, "dom"), P()),
        check_vma=False,
    )
```

```python
import functools

import jax
import jax.numpy as jnp
from jax import lax
from jax.experimental import pallas as pl
from jax.experimental.pallas import tpu as pltpu
from jax.sharding import PartitionSpec as P

DEGREE = 4
FIRST_CENTRE = -0.5
MESH = pl.DeviceIdType.MESH
f32 = jnp.float32
bf16 = jnp.bfloat16


def nt_dot(a, b):
    return lax.dot_general(a, b, (((1,), (1,)), ((), ())), preferred_element_type=f32)


def kernel(
    n,
    group,
    total_rows,
    ints,
    floats,
    vec_ref,
    diag_hbm,
    pair_hbm,
    halo_hbm,
    basis_ref,
    ritz_ref,
    tiles,
    halo_tiles,
    y_buf,
    image,
    partial,
    halo_part,
    halo_sum,
    stage,
    arrived_even,
    arrived_odd,
    far_out,
    near_out,
    far_in_a,
    near_in_a,
    far_in_b,
    near_in_b,
    load_sem,
    send_sem,
    recv_sem,
    far_send,
    near_send,
    far_recv,
    near_recv,
):
    me = lax.axis_index("dom")
    k, width = vec_ref.shape
    blocks = y_buf.shape[1]
    b = width // blocks
    entries = tiles.shape[0]
    pairs2 = entries - blocks
    groups = n // group
    bits = n.bit_length() - 1
    if n != 1 << bits:
        raise ValueError(n)
    flips = [(1 << t) * (1 - 2 * lax.rem(lax.div(me, 1 << t), 2)) for t in range(bits)]

    def partner(s):
        peer = me
        for t in range(bits):
            peer = peer + lax.rem(lax.div(s, 1 << t), 2) * flips[t]
        return peer

    at = 0

    def table(size):
        nonlocal at
        first = at
        at += size
        return lambda e: ints[first + e]

    tile_id, source_id, end_of = table(entries), table(entries), table(blocks)
    send_rows, halo_order, halo_end = table(n), table(n), table(blocks)

    def keep(e):
        return floats[e]

    def halo_keep(e):
        return floats[entries + e]

    def halo_any(r):
        return floats[entries + n + r]

    loads = [
        pltpu.make_async_copy(diag_hbm, tiles.at[pl.ds(0, blocks)], load_sem.at[0]),
        pltpu.make_async_copy(pair_hbm, tiles.at[pl.ds(blocks, pairs2)], load_sem.at[1]),
        pltpu.make_async_copy(halo_hbm, halo_tiles, load_sem.at[2]),
    ]
    for load in loads:
        load.start()

    barrier = pltpu.get_barrier_semaphore()

    def greet(s, _):
        pl.semaphore_signal(
            barrier, inc=1, device_id=(lax.rem(me + s, n),), device_id_type=MESH
        )
        return 0

    lax.fori_loop(1, n, greet, 0)
    for j in range(blocks):
        y_buf[0, j] = vec_ref[:, j * b : (j + 1) * b]
    pl.semaphore_wait(barrier, n - 1)

    slots = (arrived_even, arrived_odd)

    def halo_copy(slot, peer_from, peer_to):
        return pltpu.make_async_remote_copy(
            src_ref=stage.at[peer_to],
            dst_ref=slots[slot].at[peer_from],
            send_sem=send_sem.at[peer_to],
            recv_sem=recv_sem.at[slot, peer_from],
            device_id=(peer_to,),
            device_id_type=MESH,
        )

    entry_unroll = next(u for u in (8, 4, 2, 1) if entries % (2 * u) == 0)
    halo_unroll = next(u for u in (8, 4, 2, 1) if n % u == 0)
    near_unroll = min(4, halo_unroll)

    def no_hook():
        return None

    def operator(count, cur, early=no_hook, middle=no_hook, late=no_hook):
        slot = count % 2
        arrived = slots[slot]
        early()

        def send(i, _):
            peer = partner(n - 1 - i)
            stage[peer] = y_buf[cur, send_rows(peer)]
            halo_copy(slot, me, peer).start()
            return 0

        lax.fori_loop(0, n - 1, send, 0)
        arrived[me] = y_buf[cur, send_rows(me)]
        if count == 0:
            for load in loads:
                load.wait()

            def flip(p, _):
                halo_tiles[p] = halo_tiles[p].T
                return 0

            lax.fori_loop(0, n, flip, 0)

        def local(i, carry):
            for u in range(entry_unroll):
                e = i * entry_unroll + u
                product = jnp.dot(
                    y_buf[cur, source_id(e)], tiles[tile_id(e)], preferred_element_type=f32
                )
                carry = carry * keep(e) + product
                partial[e] = carry
            return carry

        steps = entries // entry_unroll
        carry = lax.fori_loop(0, steps // 2, local, jnp.zeros((k, b), f32))
        middle()
        lax.fori_loop(steps // 2, steps, local, carry)
        late()

        def arrivals(i, first):
            peers = [partner(i * near_unroll + u) for u in range(first, near_unroll)]
            for peer in peers:
                halo_copy(slot, peer, peer).wait_recv()
            if first:
                peers = [me] + peers
            products = [
                jnp.dot(arrived[peer], halo_tiles[peer], preferred_element_type=f32)
                for peer in peers
            ]
            for peer, product in zip(peers, products):
                halo_part[peer] = product
            return first

        arrivals(0, 1)
        lax.fori_loop(1, n // near_unroll, lambda i, x: arrivals(i, 0), 0)

        def halo(i, carry):
            for u in range(halo_unroll):
                e = i * halo_unroll + u
                carry = carry * halo_keep(e) + halo_part[halo_order(e)]
                halo_sum[e] = carry
            return carry

        lax.fori_loop(0, n // halo_unroll, halo, jnp.zeros((k, b), f32))

        def sent(s, _):
            halo_copy(slot, me, lax.rem(me + s, n)).wait_send()
            return 0

        lax.fori_loop(1, n, sent, 0)

    def applied(r):
        return partial[end_of(r)] + halo_sum[halo_end(r)] * halo_any(r)

    def over_blocks(body, init, unroll=4):
        def step(i, carry):
            for u in range(unroll):
                carry = body(i * unroll + u, carry)
            return carry

        if blocks % unroll:
            return lax.fori_loop(0, blocks, body, init)
        return lax.fori_loop(0, blocks // unroll, step, init)

    mine, team = lax.rem(me, group), lax.div(me, group)

    class Stage:
        def __init__(self, out, into, send_sems, recv_sems, size, place, device):
            self.out, self.into, self.size = out, into, size
            self.send_sems, self.recv_sems = send_sems, recv_sems
            self.place, self.device = place, device

        def copy(self, origin, other, rows):
            return pltpu.make_async_remote_copy(
                src_ref=self.out.at[pl.ds(0, rows)],
                dst_ref=self.into.at[origin, pl.ds(0, rows)],
                send_sem=self.send_sems.at[other],
                recv_sem=self.recv_sems.at[origin],
                device_id=(self.device(other),),
                device_id_type=MESH,
            )

        def start(self, value):
            rows = value.shape[0]
            self.out[0:rows] = value
            self.into[self.place, 0:rows] = value
            for s in range(1, self.size):
                self.copy(self.place, lax.rem(self.place + s, self.size), rows).start()

        def finish(self, rows):
            for s in range(1, self.size):
                other = lax.rem(self.place + s, self.size)
                self.copy(other, other, rows).wait_recv()
            total = self.into[0, 0:rows]
            for p in range(1, self.size):
                total = total + self.into[p, 0:rows]
            for s in range(1, self.size):
                self.copy(self.place, lax.rem(self.place + s, self.size), rows).wait_send()
            return total

    def two_stages(lane_set, far_in, near_in):
        far = Stage(
            far_out.at[lane_set],
            far_in,
            far_send.at[lane_set],
            far_recv.at[lane_set],
            groups,
            team,
            lambda other: other * group + mine,
        )
        near = Stage(
            near_out.at[lane_set],
            near_in,
            near_send.at[lane_set],
            near_recv.at[lane_set],
            group,
            mine,
            lambda other: team * group + other,
        )
        return far, near

    gram_stages = two_stages(0, far_in_a, near_in_a)
    other_stages = two_stages(1, far_in_b, near_in_b)

    half = k // 2
    lane = lax.broadcasted_iota(jnp.int32, (half, 2 * k), 1)

    def pack(doubled):
        return jnp.where(lane < k, doubled[:half], doubled[half:])

    def unpack(packed):
        return jnp.concatenate([packed, pltpu.roll(packed, k, 1)], axis=0)

    def inverse_factor(gram):
        sub = 8
        lanes = lax.broadcasted_iota(jnp.int32, (sub, 2 * k), 1)
        rows = lax.broadcasted_iota(jnp.int32, (sub, 2 * k), 0)
        sub_row = lax.broadcasted_iota(jnp.int32, (sub, 1), 0)
        parts = []
        for t in range(k // sub):
            unit = (lanes == rows + (t * sub + k)).astype(f32)
            parts.append(jnp.where(lanes < k, gram[t * sub : (t + 1) * sub], unit))
        for j in range(k):
            t0, r0 = divmod(j, sub)
            row = parts[t0][r0 : r0 + 1, :]
            scaled = row / row[:, j : j + 1]
            for t in range(t0, k // sub):
                column = parts[t][:, j : j + 1]
                if t == t0:
                    column = jnp.where(sub_row > r0, column, 0.0)
                parts[t] = parts[t] - column * scaled
        for t in range(k // sub):
            pivot = jnp.sum(
                jnp.where(lanes == rows + t * sub, parts[t], 0.0), axis=1, keepdims=True
            )
            parts[t] = parts[t] * lax.rsqrt(pivot)
        return pltpu.roll(jnp.concatenate(parts, axis=0), k, 1)[:, :k]

    def split(value):
        high = value.astype(bf16)
        rest = value - high.astype(f32)
        middle = rest.astype(bf16)
        return high, middle, (rest - middle.astype(f32)).astype(bf16)

    def recur(count, previous, current, following, centre):
        operator(count, current)

        def update(r, _):
            value = 2.0 * (applied(r) - centre * y_buf[current, r].astype(f32))
            value = value - y_buf[previous, r].astype(f32)
            y_buf[following, r] = value.astype(bf16)
            return 0

        over_blocks(update, 0)

    def orthonormal_image(count, current, result, visit, init):
        held = []

        def early():
            def gram_term(r, acc):
                block = y_buf[current, r]
                return acc + nt_dot(block, jnp.concatenate([block, block], axis=0))

            doubled = over_blocks(gram_term, jnp.zeros((k, 2 * k), f32))
            gram_stages[0].start(pack(doubled))

        def middle():
            gram_stages[1].start(gram_stages[0].finish(half))

        def late():
            gram = unpack(gram_stages[1].finish(half)) / total_rows
            held.extend(split(inverse_factor(gram)))

        operator(count, current, early, middle, late)
        w1, w2, w3 = held
        left = jnp.concatenate([w1, w2, w3], axis=1)
        left_image = jnp.concatenate([w1, w2, w3, w1, w2, w1], axis=1)

        def each(r, acc):
            block = y_buf[current, r]
            stacked = jnp.concatenate([block, block, block], axis=0)
            after = jnp.dot(left, stacked, preferred_element_type=f32).astype(bf16)
            y_buf[result, r] = after
            a1, a2, a3 = split(applied(r))
            right = jnp.concatenate([a1, a1, a1, a2, a2, a3], axis=0)
            return visit(r, after, jnp.dot(left_image, right, preferred_element_type=f32), acc)

        return over_blocks(each, init)

    operator(0, 0)

    def first_update(r, _):
        value = applied(r) - FIRST_CENTRE * y_buf[0, r].astype(f32)
        y_buf[1, r] = value.astype(bf16)
        return 0

    over_blocks(first_update, 0)
    count = 1
    order = [0, 1, 2]
    for _ in range(DEGREE - 1):
        recur(count, *order, FIRST_CENTRE)
        order = order[1:] + order[:1]
        count += 1
    current, result, rounded = order[1], order[2], order[0]

    def keep_image(r, after, value, acc):
        image[r] = value
        y_buf[rounded, r] = value.astype(bf16)
        return acc + value * after.astype(f32)

    traced = orthonormal_image(count, current, result, keep_image, jnp.zeros((k, b), f32))
    count += 1
    traced = sum(traced[t * 8 : (t + 1) * 8] for t in range(k // 8))
    held = []

    def trace_early():
        other_stages[0].start(traced)

    def trace_middle():
        other_stages[1].start(other_stages[0].finish(8))

    def trace_late():
        total = other_stages[1].finish(8)
        total = jnp.sum(jnp.sum(total, axis=1, keepdims=True), axis=0, keepdims=True)
        held.append(total / total_rows / k - 1.0)

    operator(count, rounded, trace_early, trace_middle, trace_late)
    count += 1
    centre = held[0]
    following = current

    def second_update(r, _):
        start = y_buf[result, r].astype(f32)
        first = image[r]
        value = first - centre * start
        y_buf[rounded, r] = value.astype(bf16)
        value = 2.0 * (applied(r) - centre * first - centre * value) - start
        y_buf[following, r] = value.astype(bf16)
        return 0

    over_blocks(second_update, 0)
    order = [rounded, following, result]
    for _ in range(DEGREE - 2):
        recur(count, *order, centre)
        order = order[1:] + order[:1]
        count += 1
    current, result = order[1], order[2]

    def ritz_term(r, after, value, acc):
        top = value.astype(bf16)
        bottom = (value - top.astype(f32)).astype(bf16)
        return acc + nt_dot(after, jnp.concatenate([top, bottom], axis=0))

    doubled = orthonormal_image(count, current, result, ritz_term, jnp.zeros((k, 2 * k), f32))
    doubled = doubled + pltpu.roll(doubled, k, 1)
    other_stages[0].start(pack(doubled))
    for j in range(blocks):
        basis_ref[:, j * b : (j + 1) * b] = y_buf[result, j]
    other_stages[1].start(other_stages[0].finish(half))
    ritz_ref[...] = unpack(other_stages[1].finish(half))[:, :k] / total_rows


def sorted_order(keys):
    count = keys.shape[0]
    ids = jnp.arange(count)
    before = (keys[None, :] < keys[:, None]) | (
        (keys[None, :] == keys[:, None]) & (ids[None, :] < ids[:, None])
    )
    rank = jnp.sum(before.astype(jnp.int32), axis=1)
    return (rank[:, None] == ids[None, :]).astype(jnp.int32)


def place(onehot, values):
    return jnp.sum(onehot * values[:, None], axis=0).astype(jnp.int32)


def local(vectors, diag_tiles, pair_tiles, halo_tiles, halo_rows, pair_index, pair_count):
    n = lax.axis_size("dom")
    k, width = vectors.shape
    blocks, b = diag_tiles.shape[0], diag_tiles.shape[1]
    pairs = pair_tiles.shape[0]
    entries = blocks + 2 * pairs
    row_ids, col_ids = pair_index[0, :, 0], pair_index[0, :, 1]
    live = jnp.arange(pairs) < pair_count[0]
    block_ids = jnp.arange(blocks)
    pair_ids = jnp.arange(pairs)
    target = jnp.concatenate(
        [block_ids, jnp.where(live, row_ids, blocks), jnp.where(live, col_ids, blocks)]
    )
    source = jnp.concatenate([block_ids, col_ids, row_ids])
    tile = jnp.concatenate([block_ids, blocks + 2 * pair_ids + 1, blocks + 2 * pair_ids])
    onehot = sorted_order(target)
    tile_id, source_id = place(onehot, tile), place(onehot, source)
    keep = (tile_id >= blocks).astype(f32)
    end_of = jnp.sum((target[None, :] <= block_ids[:, None]).astype(jnp.int32), axis=1) - 1
    rows = halo_rows[0]
    halo_onehot = sorted_order(rows)
    halo_order = place(halo_onehot, jnp.arange(n))
    halo_sorted = place(halo_onehot, rows)
    halo_keep = jnp.concatenate(
        [jnp.zeros((1,), f32), (halo_sorted[1:] == halo_sorted[:-1]).astype(f32)]
    )
    upto = jnp.sum((rows[None, :] <= block_ids[:, None]).astype(jnp.int32), axis=1)
    halo_any = jnp.any(rows[None, :] == block_ids[:, None], axis=1).astype(f32)
    halo_end = jnp.maximum(upto - 1, 0)

    ints = jnp.concatenate([tile_id, source_id, end_of, rows, halo_order, halo_end])
    floats = jnp.concatenate([keep, halo_keep, halo_any])
    group = next(g for g in (8, 4, 2, 1) if n % g == 0)
    piece = (k // 2, 2 * k)

    smem = pl.BlockSpec(memory_space=pltpu.SMEM)
    vmem = pl.BlockSpec(memory_space=pltpu.VMEM)
    hbm = pl.BlockSpec(memory_space=pl.ANY)
    return pl.pallas_call(
        functools.partial(kernel, n, group, float(width * n)),
        out_shape=(
            jax.ShapeDtypeStruct((k, width), bf16),
            jax.ShapeDtypeStruct((k, k), f32),
        ),
        in_specs=[smem] * 2 + [vmem, hbm, hbm, hbm],
        out_specs=(vmem, vmem),
        scratch_shapes=[
            pltpu.VMEM((entries, b, b), bf16),
            pltpu.VMEM((n, b, b), bf16),
            pltpu.VMEM((3, blocks, k, b), bf16),
            pltpu.VMEM((blocks, k, b), f32),
            pltpu.VMEM((entries, k, b), f32),
            pltpu.VMEM((n, k, b), f32),
            pltpu.VMEM((n, k, b), f32),
            pltpu.VMEM((n, k, b), bf16),
            pltpu.VMEM((n, k, b), bf16),
            pltpu.VMEM((n, k, b), bf16),
            pltpu.VMEM((2, *piece), f32),
            pltpu.VMEM((2, *piece), f32),
            pltpu.VMEM((n // group, *piece), f32),
            pltpu.VMEM((group, *piece), f32),
            pltpu.VMEM((n // group, *piece), f32),
            pltpu.VMEM((group, *piece), f32),
            pltpu.SemaphoreType.DMA((3,)),
            pltpu.SemaphoreType.DMA((n,)),
            pltpu.SemaphoreType.DMA((2, n)),
            pltpu.SemaphoreType.DMA((2, n // group)),
            pltpu.SemaphoreType.DMA((2, group)),
            pltpu.SemaphoreType.DMA((2, n // group)),
            pltpu.SemaphoreType.DMA((2, group)),
        ],
        compiler_params=pltpu.CompilerParams(
            collective_id=0, has_side_effects=True, vmem_limit_bytes=48 * 1024 * 1024
        ),
    )(
        ints,
        floats,
        vectors,
        diag_tiles,
        pair_tiles.reshape(2 * pairs, b, b),
        halo_tiles,
    )


def solution(mesh):
    return jax.shard_map(
        local,
        mesh=mesh,
        in_specs=(
            P(None, "dom"),
            P("dom", None, None),
            P("dom", None, None, None),
            P("dom", None, None),
            P("dom", None),
            P("dom", None, None),
            P("dom"),
        ),
        out_specs=(P(None, "dom"), P()),
        check_vma=False,
    )
```

```python
import functools

import jax
import jax.numpy as jnp
from jax import lax
from jax.experimental import pallas as pl
from jax.experimental.pallas import tpu as pltpu
from jax.sharding import PartitionSpec as P

DEGREE = 4
FIRST_CENTRE = -0.5
MESH = pl.DeviceIdType.MESH
f32 = jnp.float32
bf16 = jnp.bfloat16


def nt_dot(a, b):
    return lax.dot_general(a, b, (((1,), (1,)), ((), ())), preferred_element_type=f32)


def kernel(
    n,
    group,
    total_rows,
    ints,
    floats,
    vec_ref,
    diag_hbm,
    pair_hbm,
    halo_hbm,
    basis_ref,
    ritz_ref,
    tiles,
    halo_tiles,
    y_buf,
    image,
    partial,
    halo_part,
    halo_sum,
    stage,
    arrived_even,
    arrived_odd,
    far_out,
    near_out,
    far_in_a,
    near_in_a,
    far_in_b,
    near_in_b,
    load_sem,
    send_sem,
    recv_sem,
    far_send,
    near_send,
    far_recv,
    near_recv,
):
    me = lax.axis_index("dom")
    k, width = vec_ref.shape
    blocks = y_buf.shape[1]
    b = width // blocks
    entries = tiles.shape[0]
    pairs2 = entries - blocks
    groups = n // group
    bits = n.bit_length() - 1
    if n != 1 << bits:
        raise ValueError(n)
    flips = [(1 << t) * (1 - 2 * lax.rem(lax.div(me, 1 << t), 2)) for t in range(bits)]

    low_bits = min(3, bits)
    chunk = 1 << low_bits

    def partners(high, lows):
        base = me
        if not isinstance(high, int) or high:
            for t in range(low_bits, bits):
                scaled = lax.div(high, 1 << (t - low_bits))
                base = base + lax.rem(scaled, 2) * flips[t]
        for low in lows:
            peer = base
            for t in range(low_bits):
                if low >> t & 1:
                    peer = peer + flips[t]
            yield high * chunk + low, peer

    at = 0

    def table(size):
        nonlocal at
        first = at
        at += size
        return lambda e: ints[first + e]

    tile_id, source_id, end_of = table(entries), table(entries), table(blocks)
    send_rows, halo_order, halo_end = table(n), table(n), table(blocks)

    def keep(e):
        return floats[e]

    def halo_keep(e):
        return floats[entries + e]

    def halo_any(r):
        return floats[entries + n + r]

    loads = [
        pltpu.make_async_copy(diag_hbm, tiles.at[pl.ds(0, blocks)], load_sem.at[0]),
        pltpu.make_async_copy(pair_hbm, tiles.at[pl.ds(blocks, pairs2)], load_sem.at[1]),
        pltpu.make_async_copy(halo_hbm, halo_tiles, load_sem.at[2]),
    ]
    for load in loads:
        load.start()

    barrier = pltpu.get_barrier_semaphore()

    def greet(s, _):
        pl.semaphore_signal(
            barrier, inc=1, device_id=(lax.rem(me + s, n),), device_id_type=MESH
        )
        return 0

    lax.fori_loop(1, n, greet, 0)
    for j in range(blocks):
        y_buf[0, j] = vec_ref[:, j * b : (j + 1) * b]
    pl.semaphore_wait(barrier, n - 1)

    slots = (arrived_even, arrived_odd)

    def halo_copy(slot, s, peer):
        return pltpu.make_async_remote_copy(
            src_ref=stage.at[s],
            dst_ref=slots[slot].at[s],
            send_sem=send_sem.at[s],
            recv_sem=recv_sem.at[slot, s],
            device_id=(peer,),
            device_id_type=MESH,
        )

    entry_unroll = next(u for u in (8, 4, 2, 1) if entries % (2 * u) == 0)
    halo_unroll = next(u for u in (8, 4, 2, 1) if n % u == 0)

    def no_hook():
        return None

    def operator(count, cur, early=no_hook, middle=no_hook, late=no_hook):
        slot = count % 2
        arrived = slots[slot]
        early()

        def send(high, first):
            for s, peer in partners(high, range(chunk - 1, first - 1, -1)):
                stage[s] = y_buf[cur, send_rows(peer)]
                halo_copy(slot, s, peer).start()

        def send_high(i, _):
            send(n // chunk - 1 - i, 0)
            return 0

        lax.fori_loop(0, n // chunk - 1, send_high, 0)
        send(0, 1)
        arrived[0] = y_buf[cur, send_rows(me)]
        if count == 0:
            for load in loads:
                load.wait()

            def flip(p, _):
                halo_tiles[p] = halo_tiles[p].T
                return 0

            lax.fori_loop(0, n, flip, 0)

        def local(i, carry):
            for u in range(entry_unroll):
                e = i * entry_unroll + u
                product = jnp.dot(
                    y_buf[cur, source_id(e)], tiles[tile_id(e)], preferred_element_type=f32
                )
                carry = carry * keep(e) + product
                partial[e] = carry
            return carry

        steps = entries // entry_unroll
        carry = lax.fori_loop(0, steps // 2, local, jnp.zeros((k, b), f32))
        middle()
        lax.fori_loop(steps // 2, steps, local, carry)
        late()

        def arrivals(high, first):
            steps = list(partners(high, range(chunk)))
            for s, peer in steps[first:]:
                halo_copy(slot, s, peer).wait_recv()
            for s, peer in steps:
                halo_part[peer] = jnp.dot(
                    arrived[s], halo_tiles[peer], preferred_element_type=f32
                )

        def arrivals_high(i, _):
            arrivals(i, 0)
            return 0

        arrivals(0, 1)
        lax.fori_loop(1, n // chunk, arrivals_high, 0)

        def halo(i, carry):
            for u in range(halo_unroll):
                e = i * halo_unroll + u
                carry = carry * halo_keep(e) + halo_part[halo_order(e)]
                halo_sum[e] = carry
            return carry

        lax.fori_loop(0, n // halo_unroll, halo, jnp.zeros((k, b), f32))

        for s in range(1, n):
            halo_copy(slot, s, me + flips[0]).wait_send()

    def applied(r):
        return partial[end_of(r)] + halo_sum[halo_end(r)] * halo_any(r)

    def over_blocks(body, init, unroll=4):
        def step(i, carry):
            for u in range(unroll):
                carry = body(i * unroll + u, carry)
            return carry

        if blocks % unroll:
            return lax.fori_loop(0, blocks, body, init)
        return lax.fori_loop(0, blocks // unroll, step, init)

    mine, team = lax.rem(me, group), lax.div(me, group)

    class Stage:
        def __init__(self, out, into, send_sems, recv_sems, size, place, device):
            self.out, self.into, self.size = out, into, size
            self.send_sems, self.recv_sems = send_sems, recv_sems
            self.place, self.device = place, device

        def copy(self, origin, other, rows):
            return pltpu.make_async_remote_copy(
                src_ref=self.out.at[pl.ds(0, rows)],
                dst_ref=self.into.at[origin, pl.ds(0, rows)],
                send_sem=self.send_sems.at[other],
                recv_sem=self.recv_sems.at[origin],
                device_id=(self.device(other),),
                device_id_type=MESH,
            )

        def start(self, value):
            rows = value.shape[0]
            self.out[0:rows] = value
            self.into[self.place, 0:rows] = value
            for s in range(1, self.size):
                self.copy(self.place, lax.rem(self.place + s, self.size), rows).start()

        def finish(self, rows):
            for s in range(1, self.size):
                other = lax.rem(self.place + s, self.size)
                self.copy(other, other, rows).wait_recv()
            total = self.into[0, 0:rows]
            for p in range(1, self.size):
                total = total + self.into[p, 0:rows]
            for s in range(1, self.size):
                self.copy(self.place, lax.rem(self.place + s, self.size), rows).wait_send()
            return total

    def two_stages(lane_set, far_in, near_in):
        far = Stage(
            far_out.at[lane_set],
            far_in,
            far_send.at[lane_set],
            far_recv.at[lane_set],
            groups,
            team,
            lambda other: other * group + mine,
        )
        near = Stage(
            near_out.at[lane_set],
            near_in,
            near_send.at[lane_set],
            near_recv.at[lane_set],
            group,
            mine,
            lambda other: team * group + other,
        )
        return far, near

    gram_stages = two_stages(0, far_in_a, near_in_a)
    other_stages = two_stages(1, far_in_b, near_in_b)

    half = k // 2
    lane = lax.broadcasted_iota(jnp.int32, (half, 2 * k), 1)

    def pack(doubled):
        return jnp.where(lane < k, doubled[:half], doubled[half:])

    def unpack(packed):
        return jnp.concatenate([packed, pltpu.roll(packed, k, 1)], axis=0)

    def inverse_factor(gram):
        sub = 8
        lanes = lax.broadcasted_iota(jnp.int32, (sub, 2 * k), 1)
        rows = lax.broadcasted_iota(jnp.int32, (sub, 2 * k), 0)
        sub_row = lax.broadcasted_iota(jnp.int32, (sub, 1), 0)
        parts = []
        for t in range(k // sub):
            unit = (lanes == rows + (t * sub + k)).astype(f32)
            parts.append(jnp.where(lanes < k, gram[t * sub : (t + 1) * sub], unit))
        for j in range(k):
            t0, r0 = divmod(j, sub)
            row = parts[t0][r0 : r0 + 1, :]
            scaled = row / row[:, j : j + 1]
            for t in range(t0, k // sub):
                column = parts[t][:, j : j + 1]
                if t == t0:
                    column = jnp.where(sub_row > r0, column, 0.0)
                parts[t] = parts[t] - column * scaled
        for t in range(k // sub):
            pivot = jnp.sum(
                jnp.where(lanes == rows + t * sub, parts[t], 0.0), axis=1, keepdims=True
            )
            parts[t] = parts[t] * lax.rsqrt(pivot)
        return pltpu.roll(jnp.concatenate(parts, axis=0), k, 1)[:, :k]

    def split(value):
        high = value.astype(bf16)
        rest = value - high.astype(f32)
        middle = rest.astype(bf16)
        return high, middle, (rest - middle.astype(f32)).astype(bf16)

    def recur(count, previous, current, following, centre):
        operator(count, current)

        def update(r, _):
            value = 2.0 * (applied(r) - centre * y_buf[current, r].astype(f32))
            value = value - y_buf[previous, r].astype(f32)
            y_buf[following, r] = value.astype(bf16)
            return 0

        over_blocks(update, 0)

    def orthonormal_image(count, current, result, visit, init):
        held = []

        def early():
            def gram_term(r, acc):
                block = y_buf[current, r]
                return acc + nt_dot(block, jnp.concatenate([block, block], axis=0))

            doubled = over_blocks(gram_term, jnp.zeros((k, 2 * k), f32))
            gram_stages[0].start(pack(doubled))

        def middle():
            gram_stages[1].start(gram_stages[0].finish(half))

        def late():
            gram = unpack(gram_stages[1].finish(half)) / total_rows
            held.extend(split(inverse_factor(gram)))

        operator(count, current, early, middle, late)
        w1, w2, w3 = held
        left = jnp.concatenate([w1, w2, w3], axis=1)
        left_image = jnp.concatenate([w1, w2, w3, w1, w2, w1], axis=1)

        def each(r, acc):
            block = y_buf[current, r]
            stacked = jnp.concatenate([block, block, block], axis=0)
            after = jnp.dot(left, stacked, preferred_element_type=f32).astype(bf16)
            y_buf[result, r] = after
            a1, a2, a3 = split(applied(r))
            right = jnp.concatenate([a1, a1, a1, a2, a2, a3], axis=0)
            return visit(r, after, jnp.dot(left_image, right, preferred_element_type=f32), acc)

        return over_blocks(each, init)

    operator(0, 0)

    def first_update(r, _):
        value = applied(r) - FIRST_CENTRE * y_buf[0, r].astype(f32)
        y_buf[1, r] = value.astype(bf16)
        return 0

    over_blocks(first_update, 0)
    count = 1
    order = [0, 1, 2]
    for _ in range(DEGREE - 1):
        recur(count, *order, FIRST_CENTRE)
        order = order[1:] + order[:1]
        count += 1
    current, result, rounded = order[1], order[2], order[0]

    def keep_image(r, after, value, acc):
        image[r] = value
        y_buf[rounded, r] = value.astype(bf16)
        return acc + value * after.astype(f32)

    traced = orthonormal_image(count, current, result, keep_image, jnp.zeros((k, b), f32))
    count += 1
    traced = sum(traced[t * 8 : (t + 1) * 8] for t in range(k // 8))
    held = []

    def trace_early():
        other_stages[0].start(traced)

    def trace_middle():
        other_stages[1].start(other_stages[0].finish(8))

    def trace_late():
        total = other_stages[1].finish(8)
        total = jnp.sum(jnp.sum(total, axis=1, keepdims=True), axis=0, keepdims=True)
        held.append(total / total_rows / k - 1.0)

    operator(count, rounded, trace_early, trace_middle, trace_late)
    count += 1
    centre = held[0]
    following = current

    def second_update(r, _):
        start = y_buf[result, r].astype(f32)
        first = image[r]
        value = first - centre * start
        y_buf[rounded, r] = value.astype(bf16)
        value = 2.0 * (applied(r) - centre * first - centre * value) - start
        y_buf[following, r] = value.astype(bf16)
        return 0

    over_blocks(second_update, 0)
    order = [rounded, following, result]
    for _ in range(DEGREE - 2):
        recur(count, *order, centre)
        order = order[1:] + order[:1]
        count += 1
    current, result = order[1], order[2]

    def ritz_term(r, after, value, acc):
        top = value.astype(bf16)
        bottom = (value - top.astype(f32)).astype(bf16)
        return acc + nt_dot(after, jnp.concatenate([top, bottom], axis=0))

    doubled = orthonormal_image(count, current, result, ritz_term, jnp.zeros((k, 2 * k), f32))
    doubled = doubled + pltpu.roll(doubled, k, 1)
    other_stages[0].start(pack(doubled))
    for j in range(blocks):
        basis_ref[:, j * b : (j + 1) * b] = y_buf[result, j]
    other_stages[1].start(other_stages[0].finish(half))
    ritz_ref[...] = unpack(other_stages[1].finish(half))[:, :k] / total_rows


def sorted_order(keys):
    count = keys.shape[0]
    ids = jnp.arange(count)
    before = (keys[None, :] < keys[:, None]) | (
        (keys[None, :] == keys[:, None]) & (ids[None, :] < ids[:, None])
    )
    rank = jnp.sum(before.astype(jnp.int32), axis=1)
    return (rank[:, None] == ids[None, :]).astype(jnp.int32)


def place(onehot, values):
    return jnp.sum(onehot * values[:, None], axis=0).astype(jnp.int32)


def local(vectors, diag_tiles, pair_tiles, halo_tiles, halo_rows, pair_index, pair_count):
    n = lax.axis_size("dom")
    k, width = vectors.shape
    blocks, b = diag_tiles.shape[0], diag_tiles.shape[1]
    pairs = pair_tiles.shape[0]
    entries = blocks + 2 * pairs
    row_ids, col_ids = pair_index[0, :, 0], pair_index[0, :, 1]
    live = jnp.arange(pairs) < pair_count[0]
    block_ids = jnp.arange(blocks)
    pair_ids = jnp.arange(pairs)
    target = jnp.concatenate(
        [block_ids, jnp.where(live, row_ids, blocks), jnp.where(live, col_ids, blocks)]
    )
    source = jnp.concatenate([block_ids, col_ids, row_ids])
    tile = jnp.concatenate([block_ids, blocks + 2 * pair_ids + 1, blocks + 2 * pair_ids])
    onehot = sorted_order(target)
    tile_id, source_id = place(onehot, tile), place(onehot, source)
    keep = (tile_id >= blocks).astype(f32)
    end_of = jnp.sum((target[None, :] <= block_ids[:, None]).astype(jnp.int32), axis=1) - 1
    rows = halo_rows[0]
    halo_onehot = sorted_order(rows)
    halo_order = place(halo_onehot, jnp.arange(n))
    halo_sorted = place(halo_onehot, rows)
    halo_keep = jnp.concatenate(
        [jnp.zeros((1,), f32), (halo_sorted[1:] == halo_sorted[:-1]).astype(f32)]
    )
    upto = jnp.sum((rows[None, :] <= block_ids[:, None]).astype(jnp.int32), axis=1)
    halo_any = jnp.any(rows[None, :] == block_ids[:, None], axis=1).astype(f32)
    halo_end = jnp.maximum(upto - 1, 0)

    ints = jnp.concatenate([tile_id, source_id, end_of, rows, halo_order, halo_end])
    floats = jnp.concatenate([keep, halo_keep, halo_any])
    group = next(g for g in (8, 4, 2, 1) if n % g == 0)
    piece = (k // 2, 2 * k)

    smem = pl.BlockSpec(memory_space=pltpu.SMEM)
    vmem = pl.BlockSpec(memory_space=pltpu.VMEM)
    hbm = pl.BlockSpec(memory_space=pl.ANY)
    return pl.pallas_call(
        functools.partial(kernel, n, group, float(width * n)),
        out_shape=(
            jax.ShapeDtypeStruct((k, width), bf16),
            jax.ShapeDtypeStruct((k, k), f32),
        ),
        in_specs=[smem] * 2 + [vmem, hbm, hbm, hbm],
        out_specs=(vmem, vmem),
        scratch_shapes=[
            pltpu.VMEM((entries, b, b), bf16),
            pltpu.VMEM((n, b, b), bf16),
            pltpu.VMEM((3, blocks, k, b), bf16),
            pltpu.VMEM((blocks, k, b), f32),
            pltpu.VMEM((entries, k, b), f32),
            pltpu.VMEM((n, k, b), f32),
            pltpu.VMEM((n, k, b), f32),
            pltpu.VMEM((n, k, b), bf16),
            pltpu.VMEM((n, k, b), bf16),
            pltpu.VMEM((n, k, b), bf16),
            pltpu.VMEM((2, *piece), f32),
            pltpu.VMEM((2, *piece), f32),
            pltpu.VMEM((n // group, *piece), f32),
            pltpu.VMEM((group, *piece), f32),
            pltpu.VMEM((n // group, *piece), f32),
            pltpu.VMEM((group, *piece), f32),
            pltpu.SemaphoreType.DMA((3,)),
            pltpu.SemaphoreType.DMA((n,)),
            pltpu.SemaphoreType.DMA((2, n)),
            pltpu.SemaphoreType.DMA((2, n // group)),
            pltpu.SemaphoreType.DMA((2, group)),
            pltpu.SemaphoreType.DMA((2, n // group)),
            pltpu.SemaphoreType.DMA((2, group)),
        ],
        compiler_params=pltpu.CompilerParams(
            collective_id=0, has_side_effects=True, vmem_limit_bytes=60 * 1024 * 1024
        ),
    )(
        ints,
        floats,
        vectors,
        diag_tiles,
        pair_tiles.reshape(2 * pairs, b, b),
        halo_tiles,
    )


def solution(mesh):
    return jax.shard_map(
        local,
        mesh=mesh,
        in_specs=(
            P(None, "dom"),
            P("dom", None, None),
            P("dom", None, None, None),
            P("dom", None, None),
            P("dom", None),
            P("dom", None, None),
            P("dom"),
        ),
        out_specs=(P(None, "dom"), P()),
        check_vma=False,
    )
```
